32 devices in a mesh: seq: 16 (over z, y, x), head: 2 (over core).
Axes of the slice: x: 2, y: 2, z: 4, core: 2. Of those that a mesh axis runs over, the one named last changes fastest.
Arguments:
- hidden_in: float32 [1, 2048, 1024], P(None, 'seq'), may hold values from -6 to 6
- norm_gain: float32 [1024], replicated, may hold values from 0.5 to 1.5
- proj_z: bfloat16 [1024, 2048], P(None, 'head'), may hold values from -0.1875 to 0.1875
- proj_x: bfloat16 [1024, 2048], P(None, 'head'), may hold values from -0.1875 to 0.1875
- proj_bc: bfloat16 [1024, 256], replicated, may hold values from -0.1875 to 0.1875
- proj_dt: bfloat16 [1024, 32], P(None, 'head'), may hold values from -0.1875 to 0.1875
- conv_x_weight: float32 [4, 2048], P(None, 'head'), may hold values from -3 to 3
- conv_x_bias: float32 [2048], P('head'), may hold values from -3 to 3
- conv_bc_weight: float32 [4, 256], replicated, may hold values from -3 to 3
- conv_bc_bias: float32 [256], replicated, may hold values from -3 to 3
- step_bias: float32 [32], P('head'), may hold values from -6.9 to -2.25
- log_rate: float32 [32], P('head'), may hold values from 0 to 2.77
- skip_gain: float32 [32], P('head'), may hold values from 0.5 to 1.5
- gate_gain: float32 [2048], P('head'), may hold values from 0.5 to 1.5
- proj_out: bfloat16 [2048, 1024], P('head'), may hold values from -0.125 to 0.125
- out_grad: float32 [1, 2048, 1024], P(None, 'seq'), may hold values from -6 to 6
Outputs:
- hidden_out: float32 [1, 2048, 1024], P(None, 'seq')
- grad_in: float32 [1, 2048, 1024], P(None, 'seq')
- grad_norm_gain: float32 [1024], replicated
- grad_proj_z: float32 [1024, 2048], P('seq', 'head')
- grad_proj_x: float32 [1024, 2048], P('seq', 'head')
- grad_proj_bc: float32 [1024, 256], P(('seq', 'head'))
- grad_proj_dt: float32 [1024, 32], P('seq', 'head')
- grad_conv_x_weight: float32 [4, 2048], P(None, 'head')
- grad_conv_x_bias: float32 [2048], P('head')
- grad_conv_bc_weight: float32 [4, 256], replicated
- grad_conv_bc_bias: float32 [256], replicated
- grad_step_bias: float32 [32], P('head')
- grad_log_rate: float32 [32], P('head')
- grad_skip_gain: float32 [32], P('head')
- grad_gate_gain: float32 [2048], P('head')
- grad_proj_out: float32 [2048, 1024], P('head', 'seq')
The draws below stay inside these ranges and needn't reach their ends.
All inputs are finite; a program needn't handle non-finite values.
Results may differ from the reference program's by a relative error of at most 0.0099.
Values sent between devices are 32-bit elements; how exact they have to be, the bound alone decides.
No kernel may reach another device: no remote copies, remote signals or barrier semaphores. Data moves between devices by JAX's collectives and lax.ppermute only.
A program may use at most 192 MiB of HBM per device.

```python
import jax
import jax.numpy as jnp
from jax import lax

D = 1024
INNER = 2048
HEADS = 32
HEADDIM = 64
STATE = 128
CONV = 4
TOK_DEV = 128
SEQS = 1
LEN = 2048
N_SEQ = 16


def spiked(values, stream_key, source, target, shards_of, factor):
    owner, partner = [(jnp.arange(values.shape[axis_at]) // (values.shape[axis_at] // shards_of)).reshape([-1 if axis == axis_at else 1 for axis in range(values.ndim)]) for axis_at in (source, target)]
    chosen = jax.random.permutation(stream_key, shards_of)[partner]
    strong = (owner == chosen) | (owner == (partner + shards_of // 2) % shards_of)
    return jnp.where(strong, factor * values, values)


def shard_levels(stream_key, dims, split, low, high):
    loudness = 1.0
    for axis_at, parts in split:
        steps = jax.random.uniform(jax.random.fold_in(jax.random.fold_in(stream_key, 6), axis_at), (parts,), jnp.float32, low / len(split), high / len(split))
        loudness = loudness * jnp.repeat(jnp.exp(steps), dims[axis_at] // parts).reshape((-1,) + (1,) * (len(dims) - 1 - axis_at))
    return loudness


def noise(own_key, dims, scale, reach, shards=(), held_as=jnp.bfloat16):
    entries = jax.random.normal(own_key, dims, jnp.float32) * scale
    if len(shards) > 0:
        entries = shard_levels(own_key, dims, shards, -0.22, 0.18) * entries
    return jnp.clip(entries, min=-reach, max=reach).astype(held_as)


def heavy_noise(own_key, shape, scale, most, pieces, heavy, held_as=jnp.bfloat16):
    array = scale * jax.random.normal(own_key, shape, jnp.float32)
    if pieces:
        array = array * shard_levels(own_key, shape, pieces, -0.22, 0.18)
    return jnp.clip(spiked(array, jax.random.fold_in(own_key, 3), *heavy), -most, most).astype(held_as)


def setup_inputs(seed: int = 0) -> dict:
    key_of = jax.random.split(jax.random.key(seed), 17)
    return {
        "hidden_in": heavy_noise(key_of[0], (SEQS, LEN, D), 1.0, 6.0, ((1, 16),), (1, 2, 16, 2.0), jnp.float32),
        "norm_gain": jnp.clip(1.0 + 0.1 * jax.random.normal(key_of[1], (D,), jnp.float32), 0.5, 1.5),
        "proj_z": noise(key_of[2], (D, INNER), D ** -0.5, 0.1875, ((1, 2),)),
        "proj_x": noise(key_of[3], (D, INNER), D ** -0.5, 0.1875, ((1, 2),)),
        "proj_bc": noise(key_of[4], (D, 2 * STATE), D ** -0.5, 0.1875),
        "proj_dt": noise(key_of[5], (D, HEADS), D ** -0.5, 0.1875, ((1, 2),)),
        "conv_x_weight": noise(key_of[6], (CONV, INNER), CONV ** -0.5, 3.0, ((1, 2),), jnp.float32),
        "conv_x_bias": noise(key_of[7], (INNER,), 0.5, 3.0, ((0, 2),), jnp.float32),
        "conv_bc_weight": noise(key_of[8], (CONV, 2 * STATE), CONV ** -0.5, 3.0, (), jnp.float32),
        "conv_bc_bias": noise(key_of[9], (2 * STATE,), 0.5, 3.0, (), jnp.float32),
        "step_bias": jnp.clip(-6.9 + 4.65 * jax.random.uniform(key_of[10], (HEADS,), jnp.float32) ** shard_levels(key_of[10], (HEADS,), ((0, 2),), -0.2, 0.2), -6.9, -2.25),
        "log_rate": jnp.clip(2.77 * jax.random.uniform(key_of[11], (HEADS,), jnp.float32) ** shard_levels(key_of[11], (HEADS,), ((0, 2),), -0.2, 0.2), 0.0, 2.77),
        "skip_gain": jnp.clip(0.5 + 1.0 * jax.random.uniform(key_of[12], (HEADS,), jnp.float32) ** shard_levels(key_of[12], (HEADS,), ((0, 2),), -0.2, 0.2), 0.5, 1.5),
        "gate_gain": jnp.clip(1.0 + 0.1 * jax.random.normal(key_of[13], (INNER,), jnp.float32), 0.5, 1.5),
        "proj_out": noise(key_of[14], (INNER, D), INNER ** -0.5, 0.125, ((0, 2),)),
        "out_grad": heavy_noise(key_of[15], (SEQS, LEN, D), 1.0, 6.0, ((1, 16),), (1, 2, 16, 2.0), jnp.float32),
    }


EPS = 1e-05
HIGHEST = lax.Precision.HIGHEST

def matmul(left, right):
    return jnp.dot(left, right, preferred_element_type=jnp.float32)

def matmul_nt(left, right):
    return lax.dot_general(left, right, (((1,), (1,)), ((), ())), preferred_element_type=jnp.float32)

def matmul_tn(left, right):
    return lax.dot_general(left, right, (((0,), (0,)), ((), ())), preferred_element_type=jnp.float32)

def round_keep(values):
    return lax.optimization_barrier(values.astype(jnp.bfloat16)).astype(jnp.float32)

def silu_slope(values):
    logistic = jax.nn.sigmoid(values)
    return logistic * (1.0 + values * (1.0 - logistic))

def causal_conv(padded, kernel, bias_vec, length):
    result = bias_vec + kernel[0] * padded[:, 0:length]
    for offset in range(1, kernel.shape[0]):
        result = result + kernel[offset] * padded[:, offset:offset + length]
    return result

def conv_back(padded, kernel, grad_out, length):
    grad_pad = jnp.zeros_like(padded)
    kernel_rows = []
    for offset in range(kernel.shape[0]):
        kernel_rows.append(lax.optimization_barrier(jnp.sum(grad_out * padded[:, offset:offset + length], axis=(0, 1))))
        grad_pad = grad_pad.at[:, offset:offset + length].add(kernel[offset] * grad_out)
    return (grad_pad, jnp.stack(kernel_rows), lax.optimization_barrier(jnp.sum(grad_out, axis=(0, 1))))

def ssd_out(x_heads, step_size, decay_rate, b_input, c_output, state_in):
    step_rows = jnp.transpose(step_size, (0, 2, 1))
    cumulative = jnp.cumsum(step_rows * decay_rate[None, :, None], axis=2)
    length = x_heads.shape[1]
    causal_mask = (jnp.arange(length)[:, None] >= jnp.arange(length)[None, :])[None, None, :, :]
    log_gaps = cumulative[:, :, :, None] - cumulative[:, :, None, :]
    decay_mat = jnp.where(causal_mask, jnp.exp(jnp.where(causal_mask, log_gaps, 0.0)), 0.0)
    inner_prod = jnp.einsum('stn,sun->stu', c_output, b_input, precision=HIGHEST)
    weights = inner_prod[:, None, :, :] * decay_mat * step_rows[:, :, None, :]
    local_part = jnp.einsum('shtu,suhp->sthp', weights, x_heads, precision=HIGHEST)
    carried = jnp.einsum('stn,shpn->sthp', c_output, state_in, precision=HIGHEST)
    return local_part + jnp.transpose(jnp.exp(cumulative), (0, 2, 1))[:, :, :, None] * carried

def ssd_summary(x_heads, step_size, decay_rate, b_input):
    cumulative = jnp.cumsum(step_size * decay_rate, axis=1)
    totals = cumulative[:, -1, :]
    factor = jnp.exp(totals[:, None, :] - cumulative) * step_size
    states = jnp.einsum('sth,sthp,stn->shpn', factor, x_heads, b_input, precision=HIGHEST)
    return (jnp.exp(totals), states)

def forward_block(block_in, edge_in, state_in, params):
    norm_gain, proj_z, proj_x, proj_bc, proj_dt, conv_x_weight, conv_x_bias, conv_bc_weight, conv_bc_bias, step_bias, log_rate, skip_gain, gate_gain, proj_out = params
    batch, length, width = block_in.shape
    heads = step_bias.shape[0]
    inner = proj_z.shape[1]
    edge = CONV - 1
    inv_rms = lax.rsqrt(lax.optimization_barrier(jnp.mean(block_in * block_in, axis=-1, keepdims=True)) + EPS)
    normed = (block_in * inv_rms * norm_gain).astype(jnp.bfloat16)
    normed_rows = normed.reshape(batch * length, width)
    gate_pre = matmul(normed_rows, proj_z).reshape(batch, length, inner)
    x_pre = matmul(normed_rows, proj_x).reshape(batch, length, inner)
    bc_pre = matmul(normed_rows, proj_bc).reshape(batch, length, 2 * STATE)
    step_pre = matmul(normed_rows, proj_dt).reshape(batch, length, heads)
    x_padded = jnp.concatenate([edge_in[:, :, :inner], x_pre], axis=1)
    bc_padded = jnp.concatenate([edge_in[:, :, inner:], bc_pre], axis=1)
    x_conv = causal_conv(x_padded, conv_x_weight, conv_x_bias, length)
    bc_conv = causal_conv(bc_padded, conv_bc_weight, conv_bc_bias, length)
    x_heads = round_keep(jax.nn.silu(x_conv)).reshape(batch, length, heads, HEADDIM)
    bc_act = round_keep(jax.nn.silu(bc_conv))
    b_input = bc_act[:, :, :STATE]
    c_output = bc_act[:, :, STATE:]
    step_size = jax.nn.softplus(step_pre + step_bias)
    decay_rate = -jnp.exp(log_rate)
    decay_total, state_local = ssd_summary(x_heads, step_size, decay_rate, b_input)
    y_heads = ssd_out(x_heads, step_size, decay_rate, b_input, c_output, state_in) + skip_gain[:, None] * x_heads
    y_flat = y_heads.reshape(batch, length, inner)
    gated = y_flat * jax.nn.silu(gate_pre)
    gate_rms = lax.rsqrt(lax.optimization_barrier(jnp.sum(gated * gated, axis=-1, keepdims=True)) / INNER + EPS)
    gate_normed = (gated * gate_rms * gate_gain).astype(jnp.bfloat16)
    out_sum = matmul(gate_normed.reshape(batch * length, inner), proj_out).reshape(batch, length, width)
    edge_out = jnp.concatenate([x_pre[:, length - edge:], bc_pre[:, length - edge:]], axis=-1)
    return {'block_out': block_in + out_sum, 'edge_out': edge_out, 'inv_rms': inv_rms, 'normed': normed, 'gate_pre': gate_pre, 'step_pre': step_pre, 'x_padded': x_padded, 'bc_padded': bc_padded, 'x_conv': x_conv, 'bc_conv': bc_conv, 'x_heads': x_heads, 'b_input': b_input, 'c_output': c_output, 'step_size': step_size, 'decay_rate': decay_rate, 'decay_total': decay_total, 'state_local': state_local, 'y_flat': y_flat, 'gated': gated, 'gate_rms': gate_rms, 'gate_normed': gate_normed}

def backward_block(saved, block_in, block_grad, state_in, state_grad, edge_grad, params):
    norm_gain, proj_z, proj_x, proj_bc, proj_dt, conv_x_weight, conv_x_bias, conv_bc_weight, conv_bc_bias, step_bias, log_rate, skip_gain, gate_gain, proj_out = params
    batch, length, width = block_in.shape
    heads = step_bias.shape[0]
    inner = proj_z.shape[1]
    rows = batch * length
    edge = CONV - 1
    grad_bf = block_grad.astype(jnp.bfloat16).reshape(rows, width)
    normed_grad = matmul_nt(grad_bf, proj_out).reshape(batch, length, inner)
    grad_proj_out = matmul_tn(saved['gate_normed'].reshape(rows, inner), grad_bf)
    gate_hat = saved['gated'] * saved['gate_rms']
    grad_gate_gain = lax.optimization_barrier(jnp.sum(normed_grad * gate_hat, axis=(0, 1)))
    hat_grad = normed_grad * gate_gain
    hat_dot = lax.optimization_barrier(jnp.sum(hat_grad * gate_hat, axis=-1, keepdims=True))
    gated_grad = saved['gate_rms'] * (hat_grad - gate_hat * hat_dot / INNER)
    gate_pre = saved['gate_pre']
    y_grad = (gated_grad * jax.nn.silu(gate_pre)).reshape(batch, length, heads, HEADDIM)
    gate_grad = gated_grad * saved['y_flat'] * silu_slope(gate_pre)
    x_heads = saved['x_heads']
    step_size = saved['step_size']
    decay_rate = saved['decay_rate']
    b_input = saved['b_input']
    grad_skip_gain = lax.optimization_barrier(jnp.sum(y_grad * x_heads, axis=(0, 1, 3)))
    _, out_vjp = jax.vjp(ssd_out, x_heads, step_size, decay_rate, b_input, saved['c_output'], state_in)
    x_grad_a, step_grad_a, rate_grad_a, b_grad_a, c_grad, state_in_grad = out_vjp(y_grad)
    decay_grad = lax.optimization_barrier(jnp.sum(state_in * state_grad, axis=(2, 3)))
    _, sum_vjp = jax.vjp(ssd_summary, x_heads, step_size, decay_rate, b_input)
    x_grad_b, step_grad_b, rate_grad_b, b_grad_b = sum_vjp((decay_grad, state_grad))
    state_prev = state_in_grad + saved['decay_total'][:, :, None, None] * state_grad
    x_heads_grad = x_grad_a + x_grad_b + skip_gain[:, None] * y_grad
    x_conv_grad = x_heads_grad.reshape(batch, length, inner) * silu_slope(saved['x_conv'])
    bc_conv_grad = jnp.concatenate([b_grad_a + b_grad_b, c_grad], axis=-1) * silu_slope(saved['bc_conv'])
    step_pre_grad = (step_grad_a + step_grad_b) * jax.nn.sigmoid(saved['step_pre'] + step_bias)
    grad_step_bias = lax.optimization_barrier(jnp.sum(step_pre_grad, axis=(0, 1)))
    grad_log_rate = (rate_grad_a + rate_grad_b) * decay_rate
    x_pad_grad, grad_conv_x_weight, grad_conv_x_bias = conv_back(saved['x_padded'], conv_x_weight, x_conv_grad, length)
    bc_pad_grad, grad_conv_bc_weight, grad_conv_bc_bias = conv_back(saved['bc_padded'], conv_bc_weight, bc_conv_grad, length)
    send_edge = jnp.concatenate([x_pad_grad[:, :edge], bc_pad_grad[:, :edge]], axis=-1)
    x_pre_grad = x_pad_grad[:, edge:].at[:, length - edge:].add(edge_grad[:, :, :inner])
    bc_pre_grad = bc_pad_grad[:, edge:].at[:, length - edge:].add(edge_grad[:, :, inner:])
    gate_bf = gate_grad.astype(jnp.bfloat16).reshape(rows, inner)
    x_bf = x_pre_grad.astype(jnp.bfloat16).reshape(rows, inner)
    bc_bf = bc_pre_grad.astype(jnp.bfloat16).reshape(rows, 2 * STATE)
    step_bf = step_pre_grad.astype(jnp.bfloat16).reshape(rows, heads)
    normed_rows = saved['normed'].reshape(rows, width)
    in_grad = matmul_nt(gate_bf, proj_z) + matmul_nt(x_bf, proj_x) + matmul_nt(bc_bf, proj_bc) + matmul_nt(step_bf, proj_dt)
    in_grad = in_grad.reshape(batch, length, width)
    grad_proj_z = matmul_tn(normed_rows, gate_bf)
    grad_proj_x = matmul_tn(normed_rows, x_bf)
    grad_proj_bc = matmul_tn(normed_rows, bc_bf)
    grad_proj_dt = matmul_tn(normed_rows, step_bf)
    inv_rms = saved['inv_rms']
    norm_hat = block_in * inv_rms
    grad_norm_gain = lax.optimization_barrier(jnp.sum(in_grad * norm_hat, axis=(0, 1)))
    hat_in = in_grad * norm_gain
    grad_block = block_grad + inv_rms * (hat_in - norm_hat * lax.optimization_barrier(jnp.mean(hat_in * norm_hat, axis=-1, keepdims=True)))
    grads = (grad_norm_gain, grad_proj_z, grad_proj_x, grad_proj_bc, grad_proj_dt, grad_conv_x_weight, grad_conv_x_bias, grad_conv_bc_weight, grad_conv_bc_bias, grad_step_bias, grad_log_rate, grad_skip_gain, grad_gate_gain, grad_proj_out)
    return (grad_block, state_prev, send_edge, grads)

def reference(hidden_in, norm_gain, proj_z, proj_x, proj_bc, proj_dt, conv_x_weight, conv_x_bias, conv_bc_weight, conv_bc_bias, step_bias, log_rate, skip_gain, gate_gain, proj_out, out_grad):
    params = (norm_gain, proj_z, proj_x, proj_bc, proj_dt, conv_x_weight, conv_x_bias, conv_bc_weight, conv_bc_bias, step_bias, log_rate, skip_gain, gate_gain, proj_out)

    def split_blocks(values):
        return values.reshape(SEQS, N_SEQ, TOK_DEV, D).transpose(1, 0, 2, 3)

    def join_blocks(values):
        return values.transpose(1, 0, 2, 3).reshape(SEQS, N_SEQ * TOK_DEV, D)
    in_blocks = split_blocks(hidden_in)
    grad_blocks = split_blocks(out_grad)
    state_zero = jnp.zeros((SEQS, HEADS, HEADDIM, STATE), jnp.float32)
    edge_zero = jnp.zeros((SEQS, CONV - 1, INNER + 2 * STATE), jnp.float32)

    def forward_step(carry, block_in):
        state_in, edge_in = carry
        saved = forward_block(block_in, edge_in, state_in, params)
        state_out = saved['decay_total'][:, :, None, None] * state_in + saved['state_local']
        return ((state_out, saved['edge_out']), (saved['block_out'], state_in, edge_in))
    _, (out_blocks, state_list, edge_list) = lax.scan(forward_step, (state_zero, edge_zero), in_blocks)
    grads_zero = tuple((jnp.zeros(param.shape, jnp.float32) for param in params))

    def backward_step(carry, items):
        state_grad, edge_grad, running = carry
        block_in, block_grad, state_in, edge_in = items
        saved = forward_block(block_in, edge_in, state_in, params)
        grad_block, state_prev, send_edge, grads = backward_block(saved, block_in, block_grad, state_in, state_grad, edge_grad, params)
        running = tuple((total + fresh for total, fresh in zip(running, grads)))
        return ((state_prev, send_edge, running), grad_block)
    (_, _, totals), grad_list = lax.scan(backward_step, (state_zero, edge_zero, grads_zero), (in_blocks, grad_blocks, state_list, edge_list), reverse=True)
    return (join_blocks(out_blocks), join_blocks(grad_list), totals[0], totals[1], totals[2], totals[3], totals[4], totals[5], totals[6], totals[7], totals[8], totals[9], totals[10], totals[11], totals[12], totals[13])
```

```python
import functools

import jax
import jax.numpy as jnp
from jax import lax
from jax.experimental import pallas as pl
from jax.experimental.pallas import tpu as pltpu
from jax.sharding import PartitionSpec as P

INNER = 2048
HEADDIM = 64
STATE = 128
CONV = 4
EDGE = 8
LANES = 128

EPS = 1e-05
HIGHEST = lax.Precision.HIGHEST
F32 = jnp.float32
BF16 = jnp.bfloat16

NN = (((1,), (0,)), ((), ()))
NT = (((1,), (1,)), ((), ()))
TN = (((0,), (0,)), ((), ()))


def dot(left, right, dims=NN, precision=None):
    return lax.dot_general(left, right, dims, precision=precision, preferred_element_type=F32)


def call(body, outs, *args, smem=(), scratch=(), name=None, flops=0):
    moved = sum(a.size * a.dtype.itemsize for a in args)
    moved += sum(o.size * o.dtype.itemsize for o in outs)
    ins = len(args) - len(smem)
    buffers = [pltpu.VMEM(a.shape, a.dtype) for i, a in enumerate(args) if i not in smem]
    buffers += [pltpu.VMEM(o.shape, o.dtype) for o in outs]
    count = len(buffers)

    def kernel(*refs):
        given, results = refs[: len(args)], refs[len(args) : len(args) + len(outs)]
        rest = refs[len(args) + len(outs) :]
        held, sems, own = rest[:count], rest[count], rest[count + 1 :]
        sources = [r for i, r in enumerate(given) if i not in smem]
        loads = [
            pltpu.make_async_copy(r, held[k], sems.at[k]) for k, r in enumerate(sources)
        ]
        for copy in loads:
            copy.start()
        for copy in loads:
            copy.wait()
        body(*[r for i, r in enumerate(given) if i in smem], *held, *own)
        stores = [
            pltpu.make_async_copy(held[ins + k], r, sems.at[ins + k]) for k, r in enumerate(results)
        ]
        for copy in stores:
            copy.start()
        for copy in stores:
            copy.wait()

    anywhere = pl.BlockSpec(memory_space=pl.ANY)
    specs = [pl.BlockSpec(memory_space=pltpu.SMEM) if i in smem else anywhere for i in range(len(args))]
    grant = 62 * 1024 * 1024
    return pl.pallas_call(
        kernel,
        out_shape=tuple(outs),
        in_specs=specs,
        out_specs=tuple(anywhere for _ in outs),
        scratch_shapes=buffers + [pltpu.SemaphoreType.DMA((count,))] + list(scratch),
        name=name,
        compiler_params=pltpu.CompilerParams(vmem_limit_bytes=grant),
        cost_estimate=pl.CostEstimate(flops=flops, bytes_accessed=moved, transcendentals=0),
    )(*args)


def f32(*shape):
    return jax.ShapeDtypeStruct(shape, F32)


def bf16(*shape):
    return jax.ShapeDtypeStruct(shape, BF16)


def sigmoid(values):
    return 1.0 / (1.0 + jnp.exp(-values))


def silu_slope(values):
    logistic = sigmoid(values)
    return logistic * (1.0 + values * (1.0 - logistic))


def split3(values):
    high = values.astype(BF16)
    rest = values - high.astype(F32)
    mid = rest.astype(BF16)
    low = (rest - mid.astype(F32)).astype(BF16)
    return high, mid, low


def expand(values, spread):
    return dot(jnp.concatenate(split3(values), axis=1), spread)


def head_sums(values, onehot):
    high, mid, low = split3(values)
    return dot(high, onehot, NT) + dot(mid, onehot, NT) + dot(low, onehot, NT)


def row_ids(rows, cols):
    return lax.broadcasted_iota(jnp.int32, (rows, cols), 0)


def col_ids(rows, cols):
    return lax.broadcasted_iota(jnp.int32, (rows, cols), 1)


def left_kernel(ids, hid, gain, og, normed, nfull, nsend_a, nsend_b, gfull, gsend_a, gsend_b, ntr, gtr, tmp):
    n = ids.shape[0]
    h = hid[...]
    inv = lax.rsqrt(jnp.mean(h * h, axis=-1, keepdims=True) + EPS)
    nb = (h * inv * gain[...]).astype(BF16)
    normed[...] = nb
    rows = h.shape[1] // n
    quarter = h.shape[1] // 4
    for src, full, send_a, send_b, tr in (
        (nb, nfull, nsend_a, nsend_b, ntr),
        (og[...].astype(BF16), gfull, gsend_a, gsend_b, gtr),
    ):
        tr[...] = src.astype(F32).T
        for p in range(n):
            c = ids[p]
            tmp[p * rows : (p + 1) * rows, :] = tr[pl.ds(pl.multiple_of(c * rows, rows), rows), :]
        full[...] = tmp[...].astype(BF16)
        send_a[...] = tmp[2 * quarter :, :]
        send_b[0:quarter, :] = tmp[quarter : 2 * quarter, :]
        send_b[quarter:, :] = tmp[3 * quarter :, :]


def front_kernel(
    hid, edge, gain, wx, wbc, wdt, cxw, cxb, cbw, cbb, sbias, lrate, spread, eye,
    inv_o, xpad, xconv, xact, bcpad, bcconv, bcact, upre, dts, cums, cumst, dtst, etot, sloc, factor_o, xw_o,
    nb_s,
):
    length = hid.shape[0]
    heads = sbias.shape[1]
    h = hid[...]
    inv = lax.rsqrt(jnp.mean(h * h, axis=-1, keepdims=True) + EPS)
    inv_o[...] = inv
    nb_s[EDGE:, :] = h * inv * gain[...]
    e = edge[...]
    einv = lax.rsqrt(jnp.mean(e * e, axis=-1, keepdims=True) + EPS)
    nb_s[0:EDGE, :] = e * einv * gain[...]
    nb = nb_s[...].astype(BF16)
    u = dot(nb, wdt[...])[EDGE:, :] + sbias[...]
    upre[...] = u
    dt = jnp.maximum(u, 0.0) + jnp.log1p(jnp.exp(-jnp.abs(u)))
    dts[...] = dt
    rate = -jnp.exp(lrate[...])
    lower = (row_ids(length, length) >= col_ids(length, length)).astype(F32)
    cum = dot(lower, dt * rate, precision=HIGHEST)
    cums[...] = cum
    cumst[...] = dot(eye[...], cum, NT, precision=HIGHEST)
    dtst[...] = dot(eye[...], dt, NT, precision=HIGHEST)
    tot = cum[length - 1 :, :]
    etot[...] = jnp.zeros_like(etot)
    etot[:, 0:heads] = jnp.exp(tot)
    factor = jnp.exp(tot - cum) * dt
    fac = expand(factor, spread[...])
    factor_o[...] = fac
    bcpad[...] = dot(nb, wbc[...])
    conv = cbb[...] + cbw[0:1, :] * bcpad[EDGE - 3 : EDGE - 3 + length, :]
    for k in range(1, CONV):
        conv = conv + cbw[k : k + 1, :] * bcpad[EDGE - 3 + k : EDGE - 3 + k + length, :]
    bcconv[...] = conv
    bca = (conv * sigmoid(conv)).astype(BF16)
    bcact[...] = bca
    b = bca[:, 0:STATE]
    tile = 256
    for j in range(wx.shape[1] // tile):
        cols = slice(j * tile, (j + 1) * tile)
        xpad[:, cols] = dot(nb, wx[:, cols])
        conv = cxb[:, cols] + cxw[0:1, cols] * xpad[EDGE - 3 : EDGE - 3 + length, cols]
        for k in range(1, CONV):
            conv = conv + cxw[k : k + 1, cols] * xpad[EDGE - 3 + k : EDGE - 3 + k + length, cols]
        xconv[:, cols] = conv
        xb = (conv * sigmoid(conv)).astype(BF16)
        xact[:, cols] = xb
        xw = (fac[:, cols] * xb.astype(F32)).astype(BF16)
        xw_o[:, cols] = xw
        sloc[:, cols] = dot(b, xw, TN)


def scan_kernel(reverse, part, etot, spread, out, dec_s):
    n = part.shape[0]
    heads = spread.shape[0] // 3
    dec_s[...] = expand(etot[...][:, 0:heads], spread[...])

    def one(step, state):
        j = n - 1 - step if reverse else step
        out[j] = state
        return dec_s[pl.ds(j, 1), :] * state + part[j]

    lax.fori_loop(0, n, one, jnp.zeros(part.shape[1:], F32))


def local_kernel(normed, wz, gbf, wout, bcact, xact, cums, cumst, dtst, gate_pre, ngrad, yloc, mats, decs):
    length = normed.shape[0]
    gate_pre[...] = dot(normed[...], wz[...])
    bca = bcact[...]
    b, c = bca[:, 0:STATE], bca[:, STATE:]
    cb = dot(c, b, NT)
    mask = row_ids(length, length) >= col_ids(length, length)
    lane = col_ids(length, LANES)
    for j in range(xact.shape[1] // LANES):
        xp = xact[:, j * LANES : (j + 1) * LANES]
        y = None
        for half in range(2):
            head = 2 * j + half
            gap = cums[:, head : head + 1] - cumst[head : head + 1, :]
            dec = jnp.where(mask, jnp.exp(jnp.where(mask, gap, 0.0)), 0.0) * dtst[head : head + 1, :]
            m = (cb * dec).astype(BF16)
            decs[head] = dec.astype(BF16)
            mats[head] = m
            xh = jnp.where((lane < HEADDIM) == (half == 0), xp, jnp.zeros_like(xp))
            part = dot(m, xh)
            y = part if y is None else y + part
        yloc[:, j * LANES : (j + 1) * LANES] = y
    ngrad[...] = dot(gbf[...].astype(BF16), wout[...], NT)


def gate_kernel(sin, yloc, xact, bcact, cums, spread, skip, gate_pre, ngrad, ggain, yns, gated, ecum, sums):
    c = bcact[...][:, STATE:]
    ec = expand(jnp.exp(cums[...]), spread[...])
    ecum[...] = ec
    y0 = yloc[...] + ec * dot(c, sin[...].astype(BF16))
    yns[...] = y0
    gp = gate_pre[...]
    g = (y0 + skip[...] * xact[...].astype(F32)) * (gp * sigmoid(gp))
    gated[...] = g
    s1 = jnp.sum(g * g, axis=-1, keepdims=True)
    s2 = jnp.sum(ngrad[...] * ggain[...] * g, axis=-1, keepdims=True)
    lane = col_ids(g.shape[0], LANES)
    sums[...] = jnp.where(lane == 0, s1, jnp.where(lane == 1, s2, 0.0))


def turn_kernel(
    sums, other, gated, ngrad, ggain, gate_pre, yns, xact, skip, ecum, bcact,
    dsin, ygrad, dyc, gn, gn_a, gn_b, gg, gg_a, gg_b, ggg, skp,
):
    both = sums[...] + other[...]
    rms = lax.rsqrt(both[:, 0:1] / INNER + EPS)
    hat_dot = rms * both[:, 1:2]
    g = gated[...]
    hat = g * rms
    ng = ngrad[...]
    ggg[...] = jnp.sum(ng * hat, axis=0, keepdims=True)
    gate_normed = (hat * ggain[...]).astype(BF16)
    gn[...] = gate_normed
    mid = gate_normed.shape[1] // 2
    gn_a[...] = gate_normed[:, :mid].astype(F32)
    gn_b[...] = gate_normed[:, mid:].astype(F32)
    d = rms * (ng * ggain[...] - hat * hat_dot / INNER)
    gp = gate_pre[...]
    sg = sigmoid(gp)
    yg = d * (gp * sg)
    ygrad[...] = yg
    x = xact[...].astype(F32)
    skp[...] = jnp.sum(yg * x, axis=0, keepdims=True)
    dy = (yg * ecum[...]).astype(BF16)
    dyc[...] = dy
    dsin[...] = dot(bcact[...][:, STATE:], dy, TN)
    gate_grad = (d * (yns[...] + skip[...] * x) * (sg * (1.0 + gp * (1.0 - sg)))).astype(BF16)
    gg[...] = gate_grad
    gg_a[...] = gate_grad[:, :mid].astype(F32)
    gg_b[...] = gate_grad[:, mid:].astype(F32)


def back_kernel(mats, decs, ygrad, xact, bcact, dyc, sin, yns, onehot, dxloc, bc_part, diff, kloc_o):
    length = xact.shape[0]
    lane = col_ids(length, LANES)
    dcb = jnp.zeros((length, length), F32)
    for j in range(xact.shape[1] // LANES):
        cols = slice(j * LANES, (j + 1) * LANES)
        xp = xact[:, cols]
        dyp = ygrad[:, cols].astype(BF16)
        dx = None
        for half in range(2):
            head = 2 * j + half
            dyh = jnp.where((lane < HEADDIM) == (half == 0), dyp, jnp.zeros_like(dyp))
            dcb = dcb + dot(dyh, xp, NT) * decs[head].astype(F32)
            part = dot(mats[head], dyh, TN)
            dx = part if dx is None else dx + part
        dxloc[:, cols] = dx
    bca = bcact[...]
    b, c = bca[:, 0:STATE], bca[:, STATE:]
    dcbb = dcb.astype(BF16)
    bc_part[:, 0:STATE] = dot(dcbb, c, TN)
    bc_part[:, STATE:] = dot(dcbb, b) + dot(dyc[...], sin[...].astype(BF16), NT)
    rows = head_sums(ygrad[...].astype(BF16).astype(F32) * yns[...], onehot[...])
    kloc = head_sums(xact[...].astype(F32) * dxloc[...], onehot[...])
    diff[...] = rows - kloc
    kloc_o[...] = kloc


def end_kernel(
    ds, sin, bcact, factor, xw, xact, dxloc, ygrad, skip, xconv, bc_part, diff, kloc_i, upre, dts, lrate, etot,
    onehot, skp, xcg, bcg, dstep, smalls,
):
    length = xact.shape[0]
    heads = upre.shape[1]
    dsb = ds[...].astype(BF16)
    dxst = factor[...] * dot(bcact[...][:, 0:STATE], dsb)
    bcg[:, 0:STATE] = bc_part[:, 0:STATE] + dot(xw[...], dsb, NT)
    bcg[:, STATE:] = bc_part[:, STATE:]
    x = xact[...].astype(F32)
    grad = dxloc[...] + dxst + skip[...] * ygrad[...]
    xcg[...] = grad * silu_slope(xconv[...])
    kst = head_sums(x * dxst, onehot[...])
    carry = jnp.sum(sin[...] * ds[...], axis=0, keepdims=True)
    stack = jnp.concatenate([carry, skp[...], jnp.zeros((6, carry.shape[1]), F32)], axis=0)
    sums = head_sums(stack, onehot[...])
    dec = sums[0:1, :] * etot[...][:, 0:heads]
    upper = (col_ids(length, length) >= row_ids(length, length)).astype(F32)
    below = (col_ids(length, length) < row_ids(length, length)).astype(F32)
    q = (
        dot(upper, diff[...], precision=HIGHEST)
        + dot(below, kst, precision=HIGHEST)
        + dec
    )
    rate = -jnp.exp(lrate[...])
    u = upre[...]
    dt = dts[...]
    sg = sigmoid(u)
    step = rate * q * sg + (kloc_i[...] + kst) * (sg / jnp.maximum(dt, 1e-37))
    dstep[...] = step
    smalls[...] = jnp.zeros_like(smalls)
    smalls[0:1, 0:heads] = jnp.sum(step, axis=0, keepdims=True)
    smalls[1:2, 0:heads] = jnp.sum(dt * q, axis=0, keepdims=True) * rate
    smalls[2:3, 0:heads] = sums[1:2, :]


def conv_back_rows(grad, pad, weight, wide, length):
    taps = [
        jnp.sum(grad * pad[EDGE - 3 + k : EDGE - 3 + k + length, :], axis=0, keepdims=True)
        for k in range(CONV)
    ]
    back = weight[3:4, :] * grad
    for k in range(CONV - 1):
        back = back + weight[k : k + 1, :] * wide[3 - k : 3 - k + length, :]
    return back, jnp.concatenate(taps + [jnp.sum(grad, axis=0, keepdims=True)], axis=0)


def xback_kernel(xcg, nxt, xpad, cxw, xb, xb_a, xb_b, taps, wide):
    length = xcg.shape[0]
    wide[0:length, :] = xcg[...]
    wide[length:, :] = nxt[...]
    back, small = conv_back_rows(xcg[...], xpad, cxw[...], wide, length)
    rounded = back.astype(BF16)
    xb[...] = rounded
    mid = rounded.shape[1] // 2
    xb_a[...] = rounded[:, :mid].astype(F32)
    xb_b[...] = rounded[:, mid:].astype(F32)
    taps[0 : CONV + 1, :] = small
    taps[CONV + 1 :, :] = jnp.zeros((8 - CONV - 1, small.shape[1]), F32)


def bcsum_kernel(mine, other, bcconv, out):
    out[...] = (mine[...] + other[...]) * silu_slope(bcconv[...])


def bcback_kernel(bcg, nxt, bcpad, cbw, dstep, normed, bcb, taps, dtg, bcgrad, wide):
    length = bcg.shape[0]
    wide[0:length, :] = bcg[...]
    wide[length:, :] = nxt[...]
    back, small = conv_back_rows(bcg[...], bcpad, cbw[...], wide, length)
    rounded = back.astype(BF16)
    bcb[...] = rounded
    taps[0 : CONV + 1, :] = small
    taps[CONV + 1 :, :] = jnp.zeros((8 - CONV - 1, small.shape[1]), F32)
    nb = normed[...]
    dtg[...] = dot(dstep[...].astype(BF16), nb, TN)
    bcgrad[...] = dot(nb, rounded, TN)


def product_kernel(left, recv_la, recv_lb, right, recv_ra, recv_rb, keep, send_a, send_b):
    quarter = left.shape[0] // 4
    mid = right.shape[1] // 2
    la = jnp.concatenate([left[0 : 2 * quarter, :], recv_la[...].astype(BF16)], axis=1)
    ra = jnp.concatenate([right[:, :mid], recv_ra[...].astype(BF16)], axis=0)
    keep[:, :mid] = dot(la[:quarter], ra)
    send_a[...] = dot(la[quarter:], ra)
    lb = jnp.concatenate([left[0:quarter, :], left[2 * quarter : 3 * quarter, :]], axis=0)
    lb = jnp.concatenate([lb, recv_lb[...].astype(BF16)], axis=1)
    rb = jnp.concatenate([right[:, mid:], recv_rb[...].astype(BF16)], axis=0)
    keep[:, mid:] = dot(lb[:quarter], rb)
    send_b[...] = dot(lb[quarter:], rb)


def in_kernel(gg, wz, xb, wx, dstep, wdt, bcb, wbc, first, out):
    total = dot(gg[...], wz[...], NT) + dot(xb[...], wx[...], NT)
    total = total + dot(dstep[...].astype(BF16), wdt[...], NT)
    out[...] = total + first[...] * dot(bcb[...], wbc[...], NT)


def final_kernel(mine, other, hid, inv, gain, og, grad_in, gain_grad):
    grad = mine[...] + other[...]
    scale = inv[...]
    hat = hid[...] * scale
    gain_grad[...] = jnp.sum(grad * hat, axis=0, keepdims=True)
    hat_in = grad * gain[...]
    grad_in[...] = og[...] + scale * (hat_in - hat * jnp.mean(hat_in * hat, axis=-1, keepdims=True))


def out_kernel(gn, wout, out):
    out[...] = dot(gn[...], wout[...])


def partner(value, bit):
    peers = lax.axis_size("seq")
    return lax.ppermute(value, "seq", [(i, i ^ bit) for i in range(peers)])


def shifted(value, by):
    peers = lax.axis_size("seq")
    return lax.ppermute(value, "seq", [(i, i + by) for i in range(peers) if 0 <= i + by < peers])


def other_head(value):
    return lax.ppermute(value, "head", [(0, 1), (1, 0)])


def exchange(value):
    return lax.all_to_all(value, "seq", 0, 0, tiled=True)


def weight_grad(left, right, right_a, right_b):
    full, recv_la, recv_lb = left
    rows = full.shape[0]
    cols = right.shape[1]
    recv_ra, recv_rb = partner(right_a, 1), partner(right_b, 2)
    keep, send_a, send_b = call(
        product_kernel,
        [f32(rows // 4, cols), f32(rows // 4, cols // 2), f32(rows // 4, cols // 2)],
        full, recv_la, recv_lb, right, recv_ra, recv_rb,
        name="product", flops=4 * rows * cols * right.shape[0],
    )
    got_a, got_b = partner(send_a, 2), partner(send_b, 1)
    total = keep + jnp.concatenate([got_a, got_b], axis=1)
    bit = 4
    while bit < lax.axis_size("seq"):
        half = total.shape[0] // 2
        total = total[:half] + partner(total[half:], bit)
        bit *= 2
    return total


def body(
    hidden_in, norm_gain, proj_z, proj_x, proj_bc, proj_dt, conv_x_weight, conv_x_bias, conv_bc_weight,
    conv_bc_bias, step_bias, log_rate, skip_gain, gate_gain, proj_out, out_grad,
):
    batch, length, width = hidden_in.shape
    heads = step_bias.shape[0]
    inner = proj_z.shape[1]
    n = lax.axis_size("seq")
    place = lax.axis_index("seq")
    side = lax.axis_index("head")
    bits = n.bit_length() - 1
    hid = hidden_in.reshape(length, width)
    og = out_grad.reshape(length, width)
    gain = norm_gain.reshape(1, width)
    ggain = gate_gain.reshape(1, inner)
    sbias = step_bias.reshape(1, heads)
    lrate = log_rate.reshape(1, heads)
    skip = jnp.repeat(skip_gain, HEADDIM).reshape(1, inner)
    onehot = (jnp.arange(inner)[None, :] // HEADDIM == jnp.arange(heads)[:, None]).astype(BF16)
    spread = jnp.concatenate([onehot] * 3, axis=0)
    eye = jnp.eye(heads, dtype=F32)

    edge = shifted(hid[length - EDGE :], 1)

    order = [sum(((p >> (bits - 1 - b)) & 1) << b for b in range(bits)) for p in range(n)]
    ids = jnp.array(order, jnp.int32) ^ place
    normed, nfull, nsend_a, nsend_b, gfull, gsend_a, gsend_b = call(
        left_kernel,
        [bf16(length, width)] + [bf16(width, length), f32(width // 2, length), f32(width // 2, length)] * 2,
        ids, hid, gain, og,
        smem=(0,), scratch=[pltpu.VMEM((width, length), F32)] * 3, name="left",
    )
    nleft = (nfull, partner(nsend_a, 1), partner(nsend_b, 2))
    gleft = (gfull, partner(gsend_a, 1), partner(gsend_b, 2))

    (inv, xpad, xconv, xact, bcpad, bcconv, bcact, upre, dts, cums, cumst, dtst, etot, sloc, factor, xw) = call(
        front_kernel,
        [
            f32(length, 1), f32(length + EDGE, inner), f32(length, inner), bf16(length, inner),
            f32(length + EDGE, 2 * STATE), f32(length, 2 * STATE), bf16(length, 2 * STATE),
            f32(length, heads), f32(length, heads), f32(length, heads), f32(heads, length), f32(heads, length),
            f32(1, LANES), f32(STATE, inner), f32(length, inner), bf16(length, inner),
        ],
        hid, edge, gain, proj_x, proj_bc, proj_dt, conv_x_weight, conv_x_bias.reshape(1, inner),
        conv_bc_weight, conv_bc_bias.reshape(1, 2 * STATE), sbias, lrate, spread, eye,
        scratch=[pltpu.VMEM((length + EDGE, width), F32)], name="front",
        flops=2 * length * width * (inner + 2 * STATE),
    )
    etots = exchange(jnp.broadcast_to(etot.reshape(1, 1, LANES), (n, 1, LANES))).reshape(n, LANES)

    def prefix(states, reverse):
        parts = exchange(states.reshape(n, STATE // n, inner))
        (scanned,) = call(
            functools.partial(scan_kernel, reverse), [f32(n, STATE // n, inner)], parts, etots, spread,
            scratch=[pltpu.VMEM((n, inner), F32)], name="scan",
        )
        return exchange(scanned).reshape(STATE, inner)

    sin = prefix(sloc, False)
    gate_pre, ngrad, yloc, mats, decs = call(
        local_kernel,
        [f32(length, inner)] * 3 + [bf16(heads, length, length)] * 2,
        normed, proj_z, og, proj_out, bcact, xact, cums, cumst, dtst,
        name="local", flops=6 * length * width * inner,
    )
    yns, gated, ecum, sums = call(
        gate_kernel, [f32(length, inner)] * 3 + [f32(length, LANES)],
        sin, yloc, xact, bcact, cums, spread, skip, gate_pre, ngrad, ggain, name="gate",
    )
    half = inner // 2
    dsin, ygrad, dyc, gn, gn_a, gn_b, gg, gg_a, gg_b, ggg, skp = call(
        turn_kernel,
        [f32(STATE, inner), f32(length, inner), bf16(length, inner)]
        + [bf16(length, inner), f32(length, half), f32(length, half)] * 2
        + [f32(1, inner)] * 2,
        sums, other_head(sums), gated, ngrad, ggain, gate_pre, yns, xact, skip, ecum, bcact, name="turn",
    )
    ds = prefix(dsin, True)
    dxloc, bc_part, diff, kloc = call(
        back_kernel,
        [f32(length, inner), f32(length, 2 * STATE), f32(length, heads), f32(length, heads)],
        mats, decs, ygrad, xact, bcact, dyc, sin, yns, onehot, name="back", flops=6 * length * length * inner,
    )
    (out_part,) = call(out_kernel, [f32(length, width)], gn, proj_out, name="out", flops=2 * length * width * inner)
    hidden_out = hid + (out_part + other_head(out_part))
    grad_out_t = weight_grad(gleft, gn, gn_a, gn_b)
    grad_z = weight_grad(nleft, gg, gg_a, gg_b)

    xcg, bc_grad, dstep, smalls = call(
        end_kernel,
        [f32(length, inner), f32(length, 2 * STATE), f32(length, heads), f32(8, LANES)],
        ds, sin, bcact, factor, xw, xact, dxloc, ygrad, skip, xconv, bc_part, diff, kloc, upre, dts, lrate, etot,
        onehot, skp, name="end",
    )
    (bcg,) = call(bcsum_kernel, [f32(length, 2 * STATE)], bc_grad, other_head(bc_grad), bcconv, name="bcsum")
    xb, xb_a, xb_b, xtaps = call(
        xback_kernel,
        [bf16(length, inner), f32(length, half), f32(length, half), f32(8, inner)],
        xcg, shifted(xcg[:EDGE], -1), xpad, conv_x_weight,
        scratch=[pltpu.VMEM((length + EDGE, inner), F32)], name="xback",
    )
    grad_x = weight_grad(nleft, xb, xb_a, xb_b)
    bcb, bctaps, dtg, bcgrad = call(
        bcback_kernel,
        [bf16(length, 2 * STATE), f32(8, 2 * STATE), f32(heads, width), f32(width, 2 * STATE)],
        bcg, shifted(bcg[:EDGE], -1), bcpad, conv_bc_weight, dstep, normed,
        scratch=[pltpu.VMEM((length + EDGE, 2 * STATE), F32)], name="bcback",
    )
    first = (side == 0).astype(F32).reshape(1, 1)
    (in_part,) = call(
        in_kernel, [f32(length, width)], gg, proj_z, xb, proj_x, dstep, proj_dt, bcb, proj_bc, first,
        name="in", flops=4 * length * width * inner,
    )
    grad_in, gain_grad = call(
        final_kernel, [f32(length, width), f32(1, width)], in_part, other_head(in_part), hid, inv, gain, og,
        name="final",
    )

    rows = width // n
    bc_rows = lax.dynamic_index_in_dim(bcgrad.reshape(n, 2, rows // 2, 2 * STATE), side, 1, False)
    grad_bc = jnp.sum(exchange(bc_rows), axis=0)
    dt_rows = jnp.transpose(dtg.reshape(heads, n, rows), (1, 0, 2)).reshape(n, heads * rows)
    pack = jnp.concatenate(
        [
            gain_grad.reshape(-1), xtaps[: CONV + 1].reshape(-1), bctaps[: CONV + 1].reshape(-1),
            ggg.reshape(-1), smalls[:3].reshape(-1),
        ]
    )
    size = -(-pack.shape[0] // (n * LANES)) * LANES
    pack = jnp.pad(pack, (0, n * size - pack.shape[0])).reshape(n, size)
    reduced = jnp.sum(exchange(jnp.concatenate([dt_rows, pack], axis=1).reshape(n, 1, -1)), axis=0)
    grad_dt = jnp.transpose(reduced[0, : heads * rows].reshape(heads, rows))
    spreadout = jnp.broadcast_to(reduced[:, heads * rows :].reshape(1, 1, size), (n, 1, size))
    every = exchange(spreadout).reshape(-1)

    pieces = []
    at = 0
    for count in (width, CONV * inner, inner, CONV * 2 * STATE, 2 * STATE, inner, LANES, LANES, LANES):
        pieces.append(every[at : at + count])
        at += count
    g_norm, g_xw, g_xb, g_bw, g_bb, g_gate, g_step, g_rate, g_skip = pieces
    return (
        hidden_out.reshape(batch, length, width),
        grad_in.reshape(batch, length, width),
        g_norm,
        grad_z,
        grad_x,
        grad_bc,
        grad_dt,
        g_xw.reshape(CONV, inner),
        g_xb,
        g_bw.reshape(CONV, 2 * STATE),
        g_bb,
        g_step[:heads],
        g_rate[:heads],
        g_skip[:heads],
        g_gate,
        grad_out_t.T,
    )


def solution(mesh):
    placed = (
        P(None, "seq", None),
        P(),
        P(None, "head"),
        P(None, "head"),
        P(),
        P(None, "head"),
        P(None, "head"),
        P("head"),
        P(),
        P(),
        P("head"),
        P("head"),
        P("head"),
        P("head"),
        P("head", None),
        P(None, "seq", None),
    )
    return jax.shard_map(
        body,
        mesh=mesh,
        in_specs=placed,
        out_specs=(
            P(None, "seq", None),
            P(None, "seq", None),
            P(),
            P("seq", "head"),
            P("seq", "head"),
            P(("seq", "head"), None),
            P("seq", "head"),
            P(None, "head"),
            P("head"),
            P(),
            P(),
            P("head"),
            P("head"),
            P("head"),
            P("head"),
            P("head", "seq"),
        ),
        check_vma=False,
    )
```

```python
import functools

import jax
import jax.numpy as jnp
from jax import lax
from jax.experimental import pallas as pl
from jax.experimental.pallas import tpu as pltpu
from jax.sharding import PartitionSpec as P

INNER = 2048
HEADDIM = 64
STATE = 128
CONV = 4
EDGE = 8
LANES = 128

EPS = 1e-05
HIGHEST = lax.Precision.HIGHEST
F32 = jnp.float32
BF16 = jnp.bfloat16

NN = (((1,), (0,)), ((), ()))
NT = (((1,), (1,)), ((), ()))
TN = (((0,), (0,)), ((), ()))


def dot(left, right, dims=NN, precision=None):
    return lax.dot_general(left, right, dims, precision=precision, preferred_element_type=F32)


class Held:
    def __init__(self, ref, copy):
        self.ref, self.copy = ref, copy
        self.shape, self.dtype = ref.shape, ref.dtype

    def ready(self):
        if self.copy is not None:
            self.copy.wait()
            self.copy = None
        return self.ref

    def __getitem__(self, index):
        return self.ready()[index]


class Result:
    def __init__(self, ref, copy):
        self.ref, self.copy, self.started = ref, copy, False
        self.shape, self.dtype = ref.shape, ref.dtype

    def __getitem__(self, index):
        return self.ref[index]

    def __setitem__(self, index, value):
        self.ref[index] = value

    def flush(self):
        if not self.started:
            self.copy.start()
            self.started = True


def call(body, outs, *args, scratch=(), name=None, flops=0):
    moved = sum(a.size * a.dtype.itemsize for a in args)
    moved += sum(o.size * o.dtype.itemsize for o in outs)
    ins = len(args)
    buffers = [pltpu.VMEM(a.shape, a.dtype) for a in (*args, *outs)]
    count = len(buffers)

    def kernel(*refs):
        arrays, held, sems, own = refs[:count], refs[count : 2 * count], refs[2 * count], refs[2 * count + 1 :]
        given = [
            Held(held[k], pltpu.make_async_copy(arrays[k], held[k], sems.at[k])) for k in range(ins)
        ]
        for item in given:
            item.copy.start()
        results = [
            Result(held[k], pltpu.make_async_copy(held[k], arrays[k], sems.at[k])) for k in range(ins, count)
        ]
        body(*given, *results, *own)
        for item in given:
            item.ready()
        for item in results:
            item.flush()
        for item in results:
            item.copy.wait()

    anywhere = pl.BlockSpec(memory_space=pl.ANY)
    return pl.pallas_call(
        kernel,
        out_shape=tuple(outs),
        in_specs=[anywhere] * ins,
        out_specs=tuple(anywhere for _ in outs),
        scratch_shapes=buffers + [pltpu.SemaphoreType.DMA((count,))] + list(scratch),
        name=name,
        compiler_params=pltpu.CompilerParams(vmem_limit_bytes=62 * 1024 * 1024),
        cost_estimate=pl.CostEstimate(flops=flops, bytes_accessed=moved, transcendentals=0),
    )(*args)


def f32(*shape):
    return jax.ShapeDtypeStruct(shape, F32)


def bf16(*shape):
    return jax.ShapeDtypeStruct(shape, BF16)


def sigmoid(values):
    return 1.0 / (1.0 + jnp.exp(-values))


def silu_slope(values):
    logistic = sigmoid(values)
    return logistic * (1.0 + values * (1.0 - logistic))


def split3(values):
    high = values.astype(BF16)
    rest = values - high.astype(F32)
    mid = rest.astype(BF16)
    low = (rest - mid.astype(F32)).astype(BF16)
    return high, mid, low


def head_onehot(heads, inner, copies):
    rows = row_ids(copies * heads, inner) % heads
    return (col_ids(copies * heads, inner) // HEADDIM == rows).astype(F32).astype(BF16)


def expand(values, inner):
    return dot(jnp.concatenate(split3(values), axis=1), head_onehot(values.shape[1], inner, 3))


def head_sums(values, onehot):
    high, mid, low = split3(values)
    return dot(high, onehot, NT) + dot(mid, onehot, NT) + dot(low, onehot, NT)


def to_chunks(state, out):
    rows = STATE // out.shape[0]
    for j in range(out.shape[0]):
        for t in range(state.shape[1] // LANES):
            out[j, t * rows : (t + 1) * rows, :] = state[
                j * rows : (j + 1) * rows, t * LANES : (t + 1) * LANES
            ]


def from_chunks(parts, state):
    rows = STATE // parts.shape[0]
    for j in range(parts.shape[0]):
        for t in range(state.shape[1] // LANES):
            state[j * rows : (j + 1) * rows, t * LANES : (t + 1) * LANES] = parts[
                j, t * rows : (t + 1) * rows, :
            ]


def row_ids(rows, cols):
    return lax.broadcasted_iota(jnp.int32, (rows, cols), 0)


def col_ids(rows, cols):
    return lax.broadcasted_iota(jnp.int32, (rows, cols), 1)


def left_kernel(bits, hid, gain, og, normed, inv_o, nfull, nsend_a, nsend_b, gfull, gsend_a, gsend_b, tr, tmp):
    n = 1 << bits
    place = lax.axis_index("seq")
    h = hid[...]
    inv = lax.rsqrt(jnp.mean(h * h, axis=-1, keepdims=True) + EPS)
    inv_o[...] = inv
    nb = (h * inv * gain[...]).astype(BF16)
    normed[...] = nb
    rows = h.shape[1] // n
    quarter = h.shape[1] // 4
    for which, full, send_a, send_b in ((0, nfull, nsend_a, nsend_b), (1, gfull, gsend_a, gsend_b)):
        src = og[...].astype(BF16) if which else nb
        tr[...] = src.astype(F32).T
        for p in range(n):
            c = place ^ sum(((p >> (bits - 1 - b)) & 1) << b for b in range(bits))
            tmp[p * rows : (p + 1) * rows, :] = tr[pl.ds(pl.multiple_of(c * rows, rows), rows), :]
        send_a[...] = tmp[2 * quarter :, :]
        send_a.flush()
        send_b[0:quarter, :] = tmp[quarter : 2 * quarter, :]
        send_b[quarter:, :] = tmp[3 * quarter :, :]
        send_b.flush()
        full[...] = tmp[...].astype(BF16)
        full.flush()


def front_kernel(
    normed, edge, gain, wdt, sbias, lrate, wbc, cbw, cbb, cxw, cxb, wx,
    xpad, xconv, xact, bcpad, bcconv, bcact, upre, dts, cums, cumst, dtst, sloc, xw_o,
    nb_s, st_s,
):
    length = normed.shape[0]
    heads = sbias.shape[1]
    inner = wx.shape[1]
    e = edge[...]
    einv = lax.rsqrt(jnp.mean(e * e, axis=-1, keepdims=True) + EPS)
    nb_s[0:EDGE, :] = (e * einv * gain[...]).astype(BF16).astype(F32)
    nb_s[EDGE:, :] = normed[...].astype(F32)
    nb = nb_s[...].astype(BF16)
    u = dot(normed[...], wdt[...], NT) + sbias[...]
    upre[...] = u
    dt = jnp.maximum(u, 0.0) + jnp.log1p(jnp.exp(-jnp.abs(u)))
    dts[...] = dt
    rate = -jnp.exp(lrate[...])
    lower = (row_ids(length, length) >= col_ids(length, length)).astype(F32)
    cum = dot(lower, dt * rate, precision=HIGHEST)
    eye = (row_ids(heads, heads) == col_ids(heads, heads)).astype(F32)
    cums[...] = cum
    cumst[...] = dot(eye, cum, NT, precision=HIGHEST)
    dtst[...] = dot(eye, dt, NT, precision=HIGHEST)
    for item in (upre, dts, cums, cumst, dtst):
        item.flush()
    tot = cum[length - 1 :, :]
    fac = expand(jnp.exp(tot - cum) * dt, inner)
    leaving = expand(jnp.broadcast_to(jnp.exp(tot), (inner // LANES, heads)), inner)
    bcpad[...] = dot(nb, wbc[...])
    conv = cbb[...] + cbw[0:1, :] * bcpad[EDGE - 3 : EDGE - 3 + length, :]
    for k in range(1, CONV):
        conv = conv + cbw[k : k + 1, :] * bcpad[EDGE - 3 + k : EDGE - 3 + k + length, :]
    bcconv[...] = conv
    bca = (conv * sigmoid(conv)).astype(BF16)
    bcact[...] = bca
    for item in (bcpad, bcconv, bcact):
        item.flush()
    b = bca[:, 0:STATE]
    tile = 256
    for j in range(inner // tile):
        cols = slice(j * tile, (j + 1) * tile)
        xpad[:, cols] = dot(nb, wx[:, cols])
        conv = cxb[:, cols] + cxw[0:1, cols] * xpad[EDGE - 3 : EDGE - 3 + length, cols]
        for k in range(1, CONV):
            conv = conv + cxw[k : k + 1, cols] * xpad[EDGE - 3 + k : EDGE - 3 + k + length, cols]
        xconv[:, cols] = conv
        xb = (conv * sigmoid(conv)).astype(BF16)
        xact[:, cols] = xb
        xw = (fac[:, cols] * xb.astype(F32)).astype(BF16)
        xw_o[:, cols] = xw
        st_s[:, cols] = dot(b, xw, TN)
    for item in (xpad, xconv, xact, xw_o):
        item.flush()
    to_chunks(st_s, sloc)
    tiles = inner // LANES
    row = row_ids(tiles, LANES)
    packed = jnp.zeros((tiles, LANES), F32)
    for t in range(tiles):
        packed = packed + jnp.where(row == t, leaving[:, t * LANES : (t + 1) * LANES], 0.0)
    for j in range(sloc.shape[0]):
        sloc[j, sloc.shape[1] - tiles :, :] = packed


def scan_rows(parts, decs, out, reverse):
    n, rows, _ = out.shape
    tiles = decs(0).shape[0]
    each = rows // tiles

    def one(step, states):
        j = n - 1 - step if reverse else step
        dec = decs(j)
        after = []
        for t, state in enumerate(states):
            out[j, t * each : (t + 1) * each, :] = state
            after.append(dec[t : t + 1, :] * state + parts[j, t * each : (t + 1) * each, :])
        return tuple(after)

    lax.fori_loop(0, n, one, (jnp.zeros((each, LANES), F32),) * tiles)


def scan_kernel(parts, out, dec):
    ref, rows = parts.ready(), out.shape[1]
    dec[...] = ref[:, rows:, :]
    dec.flush()
    scan_rows(ref, lambda j: dec[j], out, False)


def scan_back_kernel(parts, dec, out):
    ref, decs = parts.ready(), dec.ready()
    scan_rows(ref, lambda j: decs[j], out, True)


def local_kernel(cums, cumst, dtst, bcact, xact, normed, wz, gbf, wout, gate_pre, ngrad, yloc, mats, decs):
    length = normed.shape[0]
    bca = bcact[...]
    b, c = bca[:, 0:STATE], bca[:, STATE:]
    cb = dot(c, b, NT)
    mask = row_ids(length, length) >= col_ids(length, length)
    lane = col_ids(length, LANES)
    for j in range(xact.shape[1] // LANES):
        xp = xact[:, j * LANES : (j + 1) * LANES]
        y = None
        for half in range(2):
            head = 2 * j + half
            gap = cums[:, head : head + 1] - cumst[head : head + 1, :]
            dec = jnp.where(mask, jnp.exp(jnp.where(mask, gap, 0.0)), 0.0) * dtst[head : head + 1, :]
            m = (cb * dec).astype(BF16)
            decs[head] = dec.astype(BF16)
            mats[head] = m
            xh = jnp.where((lane < HEADDIM) == (half == 0), xp, jnp.zeros_like(xp))
            part = dot(m, xh)
            y = part if y is None else y + part
        yloc[:, j * LANES : (j + 1) * LANES] = y
    for item in (decs, mats, yloc):
        item.flush()
    gate_pre[...] = dot(normed[...], wz[...])
    gate_pre.flush()
    ngrad[...] = dot(gbf[...].astype(BF16), wout[...], NT)


def gate_kernel(cums, skip, ggain, parts, bcact, xact, yloc, gate_pre, ngrad, sums, yns, sin, st_s):
    inner = xact.shape[1]
    from_chunks(parts.ready(), st_s)
    state = st_s[...].astype(BF16)
    sin[...] = state
    sin.flush()
    c = bcact[...][:, STATE:]
    y0 = yloc[...] + expand(jnp.exp(cums[...]), inner) * dot(c, state)
    yns[...] = y0
    yns.flush()
    gp = gate_pre[...]
    g = (y0 + expand(skip[...], inner) * xact[...].astype(F32)) * (gp * sigmoid(gp))
    s1 = jnp.sum(g * g, axis=-1, keepdims=True)
    s2 = jnp.sum(ngrad[...] * ggain[...] * g, axis=-1, keepdims=True)
    lane = col_ids(g.shape[0], LANES)
    sums[...] = jnp.where(lane == 0, s1, jnp.where(lane == 1, s2, 0.0))


def gate_values(sums, other, skip, ggain, yns, xact, gate_pre, ngrad):
    both = sums[...] + other[...]
    rms = lax.rsqrt(both[:, 0:1] / INNER + EPS)
    hat_dot = rms * both[:, 1:2]
    x = xact[...].astype(F32)
    y = yns[...] + expand(skip[...], x.shape[1]) * x
    gp = gate_pre[...]
    sg = sigmoid(gp)
    hat = y * (gp * sg) * rms
    ng = ngrad[...]
    d = rms * (ng * ggain[...] - hat * hat_dot / INNER)
    return x, y, gp, sg, hat, ng, d


def turn_kernel(sums, other, cums, skip, ggain, bcact, xact, yns, gate_pre, ngrad, dsin, dyc, ygrad, st_s):
    x, y, gp, sg, hat, ng, d = gate_values(sums, other, skip, ggain, yns, xact, gate_pre, ngrad)
    yg = d * (gp * sg)
    ygrad[...] = yg
    ygrad.flush()
    dy = (yg * expand(jnp.exp(cums[...]), x.shape[1])).astype(BF16)
    dyc[...] = dy
    dyc.flush()
    st_s[...] = dot(bcact[...][:, STATE:], dy, TN)
    to_chunks(st_s, dsin)


def turn_rest_kernel(
    sums, other, skip, ggain, xact, yns, gate_pre, ngrad, ygrad, gn, gn_a, gn_b, gg, gg_a, gg_b, ggg, skp,
):
    x, y, gp, sg, hat, ng, d = gate_values(sums, other, skip, ggain, yns, xact, gate_pre, ngrad)
    gate_normed = (hat * ggain[...]).astype(BF16)
    gn[...] = gate_normed
    mid = gate_normed.shape[1] // 2
    gn_a[...] = gate_normed[:, :mid].astype(F32)
    gn_b[...] = gate_normed[:, mid:].astype(F32)
    for item in (gn, gn_a, gn_b):
        item.flush()
    gate_grad = (d * y * (sg * (1.0 + gp * (1.0 - sg)))).astype(BF16)
    gg[...] = gate_grad
    gg_a[...] = gate_grad[:, :mid].astype(F32)
    gg_b[...] = gate_grad[:, mid:].astype(F32)
    for item in (gg, gg_a, gg_b):
        item.flush()
    ggg[...] = jnp.sum(ng * hat, axis=0, keepdims=True)
    skp[...] = jnp.sum(ygrad[...] * x, axis=0, keepdims=True)


def back_kernel(xact, ygrad, mats, decs, bcact, dyc, sin, yns, bc_part, diff, kloc_o, dxloc):
    length = xact.shape[0]
    for item in (xact, ygrad, mats, decs, bcact, dyc, sin, yns):
        item.ready()
    lane = col_ids(length, LANES)
    dcb = jnp.zeros((length, length), F32)
    for j in range(xact.shape[1] // LANES):
        cols = slice(j * LANES, (j + 1) * LANES)
        xp = xact[:, cols]
        dyp = ygrad[:, cols].astype(BF16)
        dx = None
        for half in range(2):
            head = 2 * j + half
            dyh = jnp.where((lane < HEADDIM) == (half == 0), dyp, jnp.zeros_like(dyp))
            dcb = dcb + dot(dyh, xp, NT) * decs[head].astype(F32)
            part = dot(mats[head], dyh, TN)
            dx = part if dx is None else dx + part
        dxloc[:, cols] = dx
    dxloc.flush()
    bca = bcact[...]
    b, c = bca[:, 0:STATE], bca[:, STATE:]
    dcbb = dcb.astype(BF16)
    bc_part[:, 0:STATE] = dot(dcbb, c, TN)
    bc_part[:, STATE:] = dot(dcbb, b) + dot(dyc[...], sin[...], NT)
    bc_part.flush()
    onehot = head_onehot(mats.shape[0], xact.shape[1], 1)
    rows = head_sums(ygrad[...].astype(BF16).astype(F32) * yns[...], onehot)
    kloc = head_sums(xact[...].astype(F32) * dxloc[...], onehot)
    diff[...] = rows - kloc
    kloc_o[...] = kloc


def end_kernel(
    parts, bcact, cums, dts, skip, xw, xact, dxloc, ygrad, xconv, bc_part, bcconv, sin, diff, kloc_i, upre, lrate, skp,
    xcg, bcg, edge, dstep, smalls, st_s,
):
    length, inner = xact.shape
    heads = upre.shape[1]
    from_chunks(parts.ready(), st_s)
    dsb = st_s[...].astype(BF16)
    cum = cums[...]
    dt = dts[...]
    tot = cum[length - 1 :, :]
    dxst = expand(jnp.exp(tot - cum) * dt, inner) * dot(bcact[...][:, 0:STATE], dsb)
    x = xact[...].astype(F32)
    grad = dxloc[...] + dxst + expand(skip[...], inner) * ygrad[...]
    grad = grad * silu_slope(xconv[...])
    xcg[...] = grad
    xcg.flush()
    edge[:, 0:inner] = grad[0:EDGE, :]
    slope = silu_slope(bcconv[...])
    bcg[:, 0:STATE] = (bc_part[:, 0:STATE] + dot(xw[...], dsb, NT)) * slope[:, 0:STATE]
    bcg[:, STATE:] = bc_part[:, STATE:] * slope[:, STATE:]
    bcg.flush()
    edge[:, inner:] = bcg[0:EDGE, :]
    edge.flush()
    onehot = head_onehot(heads, inner, 1)
    kst = head_sums(x * dxst, onehot)
    carry = jnp.sum(sin[...].astype(F32) * st_s[...], axis=0, keepdims=True)
    stack = jnp.concatenate([carry, skp[...], jnp.zeros((6, inner), F32)], axis=0)
    sums = head_sums(stack, onehot)
    dec = sums[0:1, :] * jnp.exp(tot)
    upper = (col_ids(length, length) >= row_ids(length, length)).astype(F32)
    below = (col_ids(length, length) < row_ids(length, length)).astype(F32)
    q = (
        dot(upper, diff[...], precision=HIGHEST)
        + dot(below, kst, precision=HIGHEST)
        + dec
    )
    rate = -jnp.exp(lrate[...])
    sg = sigmoid(upre[...])
    step = rate * q * sg + (kloc_i[...] + kst) * (sg / jnp.maximum(dt, 1e-37))
    dstep[...] = step
    smalls[...] = jnp.zeros(smalls.shape, F32)
    smalls[0:1, 0:heads] = jnp.sum(step, axis=0, keepdims=True)
    smalls[1:2, 0:heads] = jnp.sum(dt * q, axis=0, keepdims=True) * rate
    smalls[2:3, 0:heads] = sums[1:2, :]


def tap_sums(grad, pad, taps):
    length = grad.shape[0]
    for k in range(CONV):
        taps[k : k + 1, :] = jnp.sum(
            grad * pad[EDGE - 3 + k : EDGE - 3 + k + length, :], axis=0, keepdims=True
        )
    taps[CONV : CONV + 1, :] = jnp.sum(grad, axis=0, keepdims=True)
    taps[CONV + 1 :, :] = jnp.zeros((8 - CONV - 1, grad.shape[1]), F32)


def xback_kernel(nxt, xcg, cxw, xpad, xb_a, xb_b, xb, taps, wide):
    length, inner = xcg.shape
    wide[0:length, :] = xcg[...]
    wide[length:, :] = nxt[:, 0:inner]
    grad = xcg[...]
    back = cxw[3:4, :] * grad
    for k in range(CONV - 1):
        back = back + cxw[k : k + 1, :] * wide[3 - k : 3 - k + length, :]
    rounded = back.astype(BF16)
    mid = inner // 2
    xb_a[...] = rounded[:, :mid].astype(F32)
    xb_b[...] = rounded[:, mid:].astype(F32)
    xb[...] = rounded
    for item in (xb_a, xb_b, xb):
        item.flush()
    tap_sums(grad, xpad, taps)


def product_kernel(left, recv_la, recv_lb, right, recv_ra, recv_rb, send_a, send_b, far, near):
    quarter = left.shape[0] // 4
    eighth = quarter // 2
    mid = right.shape[1] // 2
    for which, recv_l, recv_r, send in ((0, recv_la, recv_ra, send_a), (1, recv_lb, recv_rb, send_b)):
        cols = slice(which * mid, which * mid + mid)
        if which == 0:
            rows = left[0 : 2 * quarter, :]
        else:
            rows = jnp.concatenate([left[0:quarter, :], left[2 * quarter : 3 * quarter, :]], axis=0)
        lhs = jnp.concatenate([rows, recv_l[...].astype(BF16)], axis=1)
        rhs = jnp.concatenate([right[:, cols], recv_r[...].astype(BF16)], axis=0)
        send[...] = dot(lhs[quarter:], rhs)
        send.flush()
        kept = dot(lhs[:quarter], rhs)
        near[:, cols] = kept[:eighth]
        far[:, cols] = kept[eighth:]


def in_kernel(
    mine, other, edge_mine, edge_other, cbw, bcpad, first, dstep, wdt, wbc, normed, gg, xb, wz, wx,
    out, bcgrad, dtg, taps, wide, full,
):
    length = mine.shape[0]
    inner = gg.shape[1]
    grad = mine[...] + other[...]
    wide[0:length, :] = grad
    wide[length:, :] = edge_mine[:, inner:] + edge_other[:, inner:]
    back = cbw[3:4, :] * grad
    for k in range(CONV - 1):
        back = back + cbw[k : k + 1, :] * wide[3 - k : 3 - k + length, :]
    bcb = back.astype(BF16)
    step = dstep[...].astype(BF16)
    total = dot(step, wdt[...]) + first[...] * dot(bcb, wbc[...], NT)
    total = total + dot(xb[...], wx[...], NT)
    out[...] = total + dot(gg[...], wz[...], NT)
    out.flush()
    nb = normed[...]
    full[...] = dot(nb, bcb, TN)
    own = lax.axis_index("head") == 0
    rows = full.shape[0] // bcgrad.shape[0]
    for c in range(bcgrad.shape[0]):
        top = full[c * rows : c * rows + rows // 2, :]
        low = full[c * rows + rows // 2 : (c + 1) * rows, :]
        bcgrad[c] = jnp.where(own, top, low)
    bcgrad.flush()
    dtg[...] = dot(step, nb, TN)
    tap_sums(grad, bcpad, taps)


def final_kernel(mine, other, hid, inv, gain, og, grad_in, gain_grad):
    grad = mine[...] + other[...]
    scale = inv[...]
    hat = hid[...] * scale
    gain_grad[...] = jnp.sum(grad * hat, axis=0, keepdims=True)
    hat_in = grad * gain[...]
    grad_in[...] = og[...] + scale * (hat_in - hat * jnp.mean(hat_in * hat, axis=-1, keepdims=True))


def out_kernel(gn, wout, out):
    out[...] = dot(gn[...], wout[...])


def partner(value, bit):
    peers = lax.axis_size("seq")
    return lax.ppermute(value, "seq", [(i, i ^ bit) for i in range(peers)])


def shifted(value, by):
    peers = lax.axis_size("seq")
    return lax.ppermute(value, "seq", [(i, i + by) for i in range(peers) if 0 <= i + by < peers])


def other_head(value):
    return lax.ppermute(value, "head", [(0, 1), (1, 0)])


def exchange(value):
    return lax.all_to_all(value, "seq", 0, 0, tiled=True)


def after(values, *others):
    return lax.optimization_barrier((values, others))[0]


def weight_start(right_a, right_b):
    return partner(right_a, 1), partner(right_b, 2)


def weight_product(left, right, recv):
    full, recv_la, recv_lb = left
    rows = full.shape[0]
    cols = right.shape[1]
    return call(
        product_kernel,
        [f32(rows // 4, cols // 2)] * 2 + [f32(rows // 8, cols)] * 2,
        full, recv_la, recv_lb, right, *recv,
        name="product", flops=4 * rows * cols * right.shape[0],
    )


def weight_second(send_a, send_b):
    return partner(send_a, 2), partner(send_b, 1)


def weight_third(far, near, got):
    got_a, got_b = got
    half = far.shape[0]
    far = far + jnp.concatenate([got_a[half:], got_b[half:]], axis=1)
    near = near + jnp.concatenate([got_a[:half], got_b[:half]], axis=1)
    return far, near


def weight_step(near, got):
    half = near.shape[0] // 2
    return near[half:] + got[half:], near[:half] + got[:half]


def weight_rest(far, near, bit):
    while 2 * bit < lax.axis_size("seq"):
        far, near = weight_step(near, partner(far, bit))
        bit *= 2
    return near + partner(far, bit)


def body(
    hidden_in, norm_gain, proj_z, proj_x, proj_bc, proj_dt, conv_x_weight, conv_x_bias, conv_bc_weight,
    conv_bc_bias, step_bias, log_rate, skip_gain, gate_gain, proj_out, out_grad,
):
    batch, length, width = hidden_in.shape
    heads = step_bias.shape[0]
    inner = proj_z.shape[1]
    n = lax.axis_size("seq")
    place = lax.axis_index("seq")
    side = lax.axis_index("head")
    bits = n.bit_length() - 1
    hid = hidden_in.reshape(length, width)
    og = out_grad.reshape(length, width)
    gain = norm_gain.reshape(1, width)
    ggain = gate_gain.reshape(1, inner)
    sbias = step_bias.reshape(1, heads)
    lrate = log_rate.reshape(1, heads)
    skip = skip_gain.reshape(1, heads)
    wdt = proj_dt.T
    tiles = inner // LANES
    chunk = (STATE // n) * tiles

    edge = shifted(hid[length - EDGE :], 1)
    normed, inv, nfull, nsend_a, nsend_b, gfull, gsend_a, gsend_b = call(
        functools.partial(left_kernel, bits),
        [bf16(length, width), f32(length, 1)]
        + [bf16(width, length), f32(width // 2, length), f32(width // 2, length)] * 2,
        hid, gain, og,
        scratch=[pltpu.VMEM((width, length), F32)] * 2, name="left",
    )
    edge, normed = lax.optimization_barrier((edge, normed))
    nleft = (nfull, partner(nsend_a, 1), partner(nsend_b, 2))
    gleft = (gfull, partner(gsend_a, 1), partner(gsend_b, 2))

    xpad, xconv, xact, bcpad, bcconv, bcact, upre, dts, cums, cumst, dtst, sloc, xw = call(
        front_kernel,
        [
            f32(length + EDGE, inner), f32(length, inner), bf16(length, inner),
            f32(length + EDGE, 2 * STATE), f32(length, 2 * STATE), bf16(length, 2 * STATE),
            f32(length, heads), f32(length, heads), f32(length, heads), f32(heads, length), f32(heads, length),
            f32(n, chunk + tiles, LANES), bf16(length, inner),
        ],
        normed, edge, gain, wdt, sbias, lrate, proj_bc, conv_bc_weight, conv_bc_bias.reshape(1, 2 * STATE),
        conv_x_weight, conv_x_bias.reshape(1, inner), proj_x,
        scratch=[pltpu.VMEM((length + EDGE, width), F32), pltpu.VMEM((STATE, inner), F32)], name="front",
        flops=2 * length * width * (inner + 2 * STATE),
    )
    parts, nleft, gleft = lax.optimization_barrier((exchange(sloc), nleft, gleft))
    scanned, decays = call(scan_kernel, [f32(n, chunk, LANES), f32(n, tiles, LANES)], parts, name="scan")
    gate_pre, ngrad, yloc, mats, decs = call(
        local_kernel,
        [f32(length, inner)] * 3 + [bf16(heads, length, length)] * 2,
        cums, cumst, dtst, bcact, xact, normed, proj_z, og, proj_out,
        name="local", flops=6 * length * width * inner,
    )
    state = pltpu.VMEM((STATE, inner), F32)
    got_states = exchange(scanned)
    sums, yns, sin = call(
        gate_kernel, [f32(length, LANES), f32(length, inner), bf16(STATE, inner)],
        cums, skip, ggain, got_states, bcact, xact, yloc, gate_pre, ngrad, scratch=[state], name="gate",
    )
    half = inner // 2
    sums_other = other_head(sums)
    dsin, dyc, ygrad = call(
        turn_kernel, [f32(n, chunk, LANES), bf16(length, inner), f32(length, inner)],
        sums, sums_other, cums, skip, ggain, bcact, xact, yns, gate_pre, ngrad, scratch=[state], name="turn",
    )
    dparts = exchange(dsin)
    gn, gn_a, gn_b, gg, gg_a, gg_b, ggg, skp = call(
        turn_rest_kernel,
        [bf16(length, inner), f32(length, half), f32(length, half)] * 2 + [f32(1, inner)] * 2,
        sums, sums_other, skip, ggain, xact, yns, gate_pre, ngrad, ygrad, name="turnrest",
    )
    bc_part, diff, kloc, dxloc = call(
        back_kernel,
        [f32(length, 2 * STATE), f32(length, heads), f32(length, heads), f32(length, inner)],
        xact, ygrad, mats, decs, bcact, dyc, sin, yns, name="back", flops=6 * length * length * inner,
    )
    (out_part,) = call(out_kernel, [f32(length, width)], gn, proj_out, name="out", flops=2 * length * width * inner)
    recv_o = weight_start(gn_a, gn_b)
    hidden_out = hid + (out_part + other_head(out_part))
    dparts, hidden_out, dxloc, recv_o = lax.optimization_barrier((dparts, hidden_out, dxloc, recv_o))
    (dscanned,) = call(scan_back_kernel, [f32(n, chunk, LANES)], dparts, decays, name="scanback")
    ds = exchange(dscanned)
    osend_a, osend_b, ofar, onear = weight_product(gleft, gn, after(recv_o, dscanned))
    got_o = weight_second(osend_a, osend_b)
    recv_z = weight_start(*after((gg_a, gg_b), osend_a))
    ds = after(ds, osend_a)

    xcg, bcg, edge_grad, dstep, smalls = call(
        end_kernel,
        [f32(length, inner), f32(length, 2 * STATE), f32(EDGE, inner + 2 * STATE), f32(length, heads), f32(8, LANES)],
        ds, bcact, cums, dts, skip, xw, xact, dxloc, ygrad, xconv, bc_part, bcconv, sin, diff, kloc, upre, lrate, skp,
        scratch=[state], name="end",
    )
    edge_next = shifted(edge_grad, -1)
    ofar, onear = weight_third(ofar, onear, after(got_o, edge_grad))
    got_o = partner(ofar, 4)
    xb_a, xb_b, xb, xtaps = call(
        xback_kernel,
        [f32(length, half), f32(length, half), bf16(length, inner), f32(8, inner)],
        edge_next, xcg, conv_x_weight, xpad,
        scratch=[pltpu.VMEM((length + EDGE, inner), F32)], name="xback",
    )
    recv_x = weight_start(xb_a, xb_b)
    zsend_a, zsend_b, zfar, znear = weight_product(nleft, gg, after(recv_z, edge_grad))
    got_z = weight_second(zsend_a, zsend_b)
    ofar, onear = weight_step(onear, after(got_o, xb))
    grad_out_t = weight_rest(ofar, onear, 8)
    first = (side == 0).astype(F32).reshape(1, 1)
    in_part, bcgrad, dtg, bctaps = call(
        in_kernel,
        [f32(length, width), f32(n, width // n // 2, 2 * STATE), f32(heads, width), f32(8, 2 * STATE)],
        after(bcg, ofar), other_head(bcg), edge_next, other_head(edge_next), conv_bc_weight, bcpad, first, dstep, wdt,
        proj_bc, normed, gg, xb, proj_z, proj_x,
        scratch=[pltpu.VMEM((length + EDGE, 2 * STATE), F32), pltpu.VMEM((width, 2 * STATE), F32)],
        name="in", flops=4 * length * width * inner,
    )
    zfar, znear = weight_third(zfar, znear, after(got_z, in_part))
    got_z = partner(zfar, 4)
    xsend_a, xsend_b, xfar, xnear = weight_product(nleft, xb, after(recv_x, zfar))
    got_x = weight_second(xsend_a, xsend_b)
    grad_in, gain_grad = call(
        final_kernel, [f32(length, width), f32(1, width)],
        in_part, other_head(in_part), after(hid, xsend_a, grad_out_t), inv, gain, og,
        name="final",
    )
    zfar, znear = weight_step(znear, after(got_z, gain_grad))

    rows = width // n
    dt_rows = jnp.transpose(dtg.reshape(heads, n, rows), (1, 0, 2)).reshape(n, heads * rows)
    pack = jnp.concatenate(
        [
            gain_grad.reshape(-1), xtaps[: CONV + 1].reshape(-1), bctaps[: CONV + 1].reshape(-1),
            ggg.reshape(-1), smalls[:3].reshape(-1),
        ]
    )
    size = -(-pack.shape[0] // (n * LANES)) * LANES
    pack = jnp.pad(pack, (0, n * size - pack.shape[0])).reshape(n, size)
    small = jnp.concatenate([dt_rows, pack], axis=1)
    wide = 2 * STATE
    lines = -(-small.shape[1] // wide)
    small = jnp.pad(small, ((0, 0), (0, lines * wide - small.shape[1]))).reshape(n, lines, wide)
    grad_z = weight_rest(zfar, znear, 8)
    reduced = jnp.sum(exchange(jnp.concatenate([bcgrad, after(small, zfar)], axis=1)), axis=0)
    xfar, xnear = weight_third(xfar, xnear, after(got_x, zfar, small))
    got_x = partner(xfar, 4)
    reduced = after(reduced, xfar)
    grad_bc = reduced[: rows // 2]
    reduced = reduced[rows // 2 :].reshape(-1)
    grad_dt = jnp.transpose(reduced[: heads * rows].reshape(heads, rows))
    spreadout = jnp.broadcast_to(
        reduced[heads * rows : heads * rows + size].reshape(1, 1, size), (n, 1, size)
    )
    every = exchange(spreadout).reshape(-1)

    xfar, xnear = weight_step(xnear, after(got_x, grad_z))
    grad_x = weight_rest(xfar, xnear, 8)
    pieces = []
    at = 0
    for count in (width, CONV * inner, inner, CONV * 2 * STATE, 2 * STATE, inner, LANES, LANES, LANES):
        pieces.append(every[at : at + count])
        at += count
    g_norm, g_xw, g_xb, g_bw, g_bb, g_gate, g_step, g_rate, g_skip = pieces
    return (
        hidden_out.reshape(batch, length, width),
        grad_in.reshape(batch, length, width),
        g_norm,
        grad_z,
        grad_x,
        grad_bc,
        grad_dt,
        g_xw.reshape(CONV, inner),
        g_xb,
        g_bw.reshape(CONV, 2 * STATE),
        g_bb,
        g_step[:heads],
        g_rate[:heads],
        g_skip[:heads],
        g_gate,
        grad_out_t.T,
    )


def solution(mesh):
    placed = (
        P(None, "seq", None),
        P(),
        P(None, "head"),
        P(None, "head"),
        P(),
        P(None, "head"),
        P(None, "head"),
        P("head"),
        P(),
        P(),
        P("head"),
        P("head"),
        P("head"),
        P("head"),
        P("head", None),
        P(None, "seq", None),
    )
    return jax.shard_map(
        body,
        mesh=mesh,
        in_specs=placed,
        out_specs=(
            P(None, "seq", None),
            P(None, "seq", None),
            P(),
            P("seq", "head"),
            P("seq", "head"),
            P(("seq", "head"), None),
            P("seq", "head"),
            P(None, "head"),
            P("head"),
            P(),
            P(),
            P("head"),
            P("head"),
            P("head"),
            P("head"),
            P("head", "seq"),
        ),
        check_vma=False,
    )
```
